512 devices in a mesh: seq: 64 (over y_lo, z, core), ch: 8 (over y_hi, x).
Axes of the slice: x: 4, y: 8 (y_hi: 2, y_lo: 4; y = y_hi * 4 + y_lo), z: 8, core: 2. Of those that a mesh axis runs over, the one named last changes fastest.
Arguments:
- grad_out: bfloat16 [16384, 4096], P('seq', 'ch'), may hold values from -6 to 6
- saved_in: bfloat16 [16384, 4096], P('seq', 'ch'), may hold values from -6 to 6
- filter_taps: bfloat16 [256, 4096], P(None, 'ch'), may hold values from -0.375 to 0.375
- skip_gain: float32 [4096], P('ch'), may hold values from 0.5 to 1.5
- projection: bfloat16 [4096, 4096], P('seq', 'ch'), may hold values from -0.09375 to 0.09375
Outputs:
- grad_in: bfloat16 [16384, 4096], P('seq', 'ch')
- filter_grad: float32 [256, 4096], P('seq', 'ch')
The draws below stay inside these ranges and needn't reach their ends.
All inputs are finite; a program needn't handle non-finite values.
Results may differ from the reference program's by a relative error of at most 0.015.
Values may be sent and summed in bfloat16 or wider, within the bound.
A program may use at most 64 MiB of HBM per device.

```python
import jax
import jax.numpy as jnp
from jax import lax

D = 4096
FILTER = 256
TOKENS = 16384
N_CH = 8


def block_levels(key, shape, cuts, smallest, high):
    gain, own = 1.0, jax.random.fold_in(key, 6)
    for position, parts in cuts:
        draws = jnp.exp(jax.random.uniform(jax.random.fold_in(own, position), (parts,), jnp.float32, smallest / len(cuts), high / len(cuts)))
        gain = gain * jnp.repeat(draws, shape[position] // parts).reshape([-1 if axis == position else 1 for axis in range(len(shape))])
    return gain


def centred(rng, shape, deviation, bound, pieces=(), held_as=jnp.bfloat16):
    array = jax.random.normal(rng, shape, jnp.float32) * deviation
    if len(pieces) > 0:
        array = block_levels(rng, shape, pieces, -0.22, 0.18) * array
    return jnp.clip(array, min=-bound, max=bound).astype(held_as)


def setup_inputs(seed: int = 0) -> dict:
    key_of = jax.random.split(jax.random.key(seed), 6)
    return {
        "grad_out": centred(key_of[0], (TOKENS, D), 1.0, 6.0, ((0, 64), (1, 8))),
        "saved_in": centred(key_of[1], (TOKENS, D), 1.0, 6.0, ((0, 64), (1, 8))),
        "filter_taps": centred(key_of[2], (FILTER, D), FILTER ** -0.5, 0.375, ((1, 8),)),
        "skip_gain": jnp.clip(0.5 + 1.0 * jax.random.uniform(key_of[3], (D,), jnp.float32) ** block_levels(key_of[3], (D,), ((0, 8),), -0.2, 0.2), 0.5, 1.5),
        "projection": centred(key_of[4], (D, D), D ** -0.5, 0.09375, ((0, 64), (1, 8))),
    }


def spectral(first, second, offset, count):
    fft_size = 1
    while fft_size < first.shape[0] + second.shape[0]:
        fft_size = fft_size * 2
    first_hat = jnp.fft.rfft(first, n=fft_size, axis=0)
    second_hat = jnp.fft.rfft(second, n=fft_size, axis=0)
    linear = jnp.fft.irfft(first_hat * second_hat, n=fft_size, axis=0)
    return linear[offset:offset + count]

def reference(grad_out, saved_in, filter_taps, skip_gain, projection):
    tap_count = filter_taps.shape[0]
    seq_length = grad_out.shape[0]
    gradient = grad_out.astype(jnp.float32)
    inputs = saved_in.astype(jnp.float32)
    taps = filter_taps.astype(jnp.float32)
    reversed_taps = taps[:, ::-1]
    block_width = min(512, D)
    conv_blocks = []
    forward_blocks = []
    mirror_blocks = []
    for block_index in range(D // block_width):
        low = block_index * block_width
        high = low + block_width
        grad_block = gradient[:, low:high]
        input_block = inputs[:, low:high]
        forward = spectral(grad_block, taps[::-1, low:high], tap_count - 1, seq_length)
        backward = spectral(grad_block, reversed_taps[:, low:high], 0, seq_length)
        conv_blocks.append(forward + backward)
        forward_blocks.append(spectral(grad_block, input_block[::-1], seq_length - 1, tap_count))
        mirror_blocks.append(spectral(input_block, grad_block[::-1], seq_length - 1, tap_count))
    conv_sum = jnp.concatenate(conv_blocks, axis=1)
    filter_sum = jnp.concatenate(forward_blocks, axis=1) + jnp.concatenate(mirror_blocks, axis=1)[:, ::-1]
    grad_conv = (conv_sum + skip_gain[None, :] * gradient).astype(jnp.bfloat16)
    shard_width = D // N_CH
    total = jnp.zeros((seq_length, D), jnp.float32)
    for shard_index in range(N_CH):
        low = shard_index * shard_width
        high = low + shard_width
        partial_value = jnp.dot(grad_conv[:, low:high], projection[:, low:high].T, preferred_element_type=jnp.float32)
        rounded = lax.optimization_barrier(partial_value.astype(jnp.bfloat16))
        total = total + rounded.astype(jnp.float32)
    grad_in = total.astype(jnp.bfloat16)
    filter_grad = filter_sum * (1.0 / jnp.sqrt(jnp.float32(TOKENS)))
    return (grad_in, filter_grad)
```

```python
import math

import jax
import jax.numpy as jnp
import ml_dtypes
import numpy as np
from jax import lax
from jax.sharding import PartitionSpec as P


def half_bin_basis(rows):
    size = 2 * rows
    angle = 2.0 * np.pi * np.outer(np.arange(rows) + 0.5, np.arange(rows)) / size
    return np.concatenate([np.cos(angle), -np.sin(angle)], axis=0)


def bf16(values):
    return jnp.asarray(values.astype(ml_dtypes.bfloat16))


def split(spectrum):
    half = spectrum.shape[0] // 2
    return spectrum[:half], spectrum[half:]


def body(grad_out, saved_in, filter_taps, skip_gain, projection):
    rows, cols = grad_out.shape
    n_seq, n_ch = lax.axis_size("seq"), lax.axis_size("ch")
    basis = half_bin_basis(rows)
    forward = bf16(basis)
    inverse = bf16(basis.T / rows)
    all_rows = lax.all_gather(projection, "seq", axis=0, tiled=True)
    mirror = [(j, n_ch - 1 - j) for j in range(n_ch)]
    later = lax.ppermute(grad_out, "seq", [(i + 1, i) for i in range(n_seq - 1)])
    earlier = lax.ppermute(grad_out, "seq", [(i, i + 1) for i in range(n_seq - 1)])
    mirror_taps = lax.ppermute(filter_taps, "ch", mirror)[:, ::-1]

    def spectrum(block):
        return split(jnp.dot(forward, block, preferred_element_type=jnp.float32))

    sign = jnp.asarray(np.where(np.arange(rows) % 2 == 0, 1.0, -1.0).astype(np.float32))[:, None]
    here_r, here_i = spectrum(grad_out)
    next_r, next_i = spectrum(later)
    prev_r, prev_i = spectrum(earlier)
    in_r, in_i = spectrum(saved_in)
    tap_r, tap_i = spectrum(filter_taps)
    mir_r, mir_i = spectrum(mirror_taps)
    up_r, up_i = here_r + sign * next_i, here_i - sign * next_r
    dn_r, dn_i = here_r - sign * prev_i, here_i + sign * prev_r
    conv_r = up_r * tap_r + up_i * tap_i + dn_r * mir_r - dn_i * mir_i
    conv_i = up_i * tap_r - up_r * tap_i + dn_r * mir_i + dn_i * mir_r
    pos_r, pos_i = in_r * up_r + in_i * up_i, in_r * up_i - in_i * up_r
    neg_r, neg_i = in_r * dn_r + in_i * dn_i, in_i * dn_r - in_r * dn_i

    def back(real, imag):
        packed = jnp.concatenate([real, imag], axis=0).astype(jnp.bfloat16)
        return jnp.dot(inverse, packed, preferred_element_type=jnp.float32)

    conv_sum = back(conv_r, conv_i)
    grad_conv = (conv_sum + skip_gain[None, :] * grad_out.astype(jnp.float32)).astype(jnp.bfloat16)
    partial_value = lax.dot_general(
        grad_conv, all_rows, (((1,), (1,)), ((), ())), preferred_element_type=jnp.float32
    )
    grad_in = lax.psum_scatter(
        partial_value.astype(jnp.bfloat16), "ch", scatter_dimension=1, tiled=True
    )
    positive = lax.psum_scatter(back(pos_r, pos_i), "seq", scatter_dimension=0, tiled=True)
    negative = lax.psum_scatter(back(neg_r, neg_i), "seq", scatter_dimension=0, tiled=True)
    mirrored = lax.ppermute(negative, "ch", mirror)[:, ::-1]
    filter_grad = (positive + mirrored) * (1.0 / math.sqrt(rows * n_seq))
    return (grad_in, filter_grad)


def solution(mesh):
    placed = (P("seq", "ch"), P("seq", "ch"), P(None, "ch"), P("ch"), P("seq", "ch"))
    return jax.shard_map(
        body,
        mesh=mesh,
        in_specs=placed,
        out_specs=(P("seq", "ch"), P("seq", "ch")),
        check_vma=False,
    )
```

```python
import math

import jax
import jax.numpy as jnp
import ml_dtypes
import numpy as np
from jax import lax
from jax.experimental import pallas as pl
from jax.experimental.pallas import tpu as pltpu
from jax.sharding import PartitionSpec as P

NY, NZ, NX = 4, 8, 4
ROWS, COLS = 256, 512
F32, BF16 = jnp.float32, jnp.bfloat16
OFFSETS = (0, -1, 1, -2, 2, -3, 3, 4)


def half_bin_basis(rows):
    angle = np.pi * np.outer(np.arange(rows) + 0.5, np.arange(rows)) / rows
    return np.concatenate([np.cos(angle), -np.sin(angle)], axis=0)


def lag_order():
    core, z, y, r = np.meshgrid(np.arange(2), np.arange(NZ), np.arange(NY), np.arange(4), indexing="ij")
    return (((y * NZ + z) * 2 + core) * 4 + r).reshape(-1)


def dot(a, b):
    return jnp.dot(a, b, preferred_element_type=F32)


def kernel(
    g_ref, x_ref, f_ref, skip_ref, p_ref, fwd_ref, inv_ref, lag_ref,
    out_ref, fg_ref,
    halo, mt, pg, sx, rx, ysend, yrecv, gc, rev,
    s_here, s_in, s_tap, s_next, s_prev, s_mir, q_conv, q_pos, q_neg,
    lags, kbuf, half_sum, zbuf, ysum, ypos, yneg,
    tap_ss, tap_rs, halo_ss, halo_rs, py_ss, py_rs, ring_ss, ring_rs, sib_ss, sib_rs, last_ss, last_rs,
    xs_ss, xs_rs, yh_ss, yh_rs, k_ss, k_rs, z_ss, z_rs, y_ss, y_rs,
):
    seq, ch = lax.axis_index("seq"), lax.axis_index("ch")
    y, z, k = seq // 16, (seq // 2) % NZ, seq % 2
    half, x = ch // NX, ch % NX

    def at(y_, z_, k_, half_, x_):
        return ((y_ * NZ + z_) * 2 + k_, half_ * NX + x_)

    def send(src, dst, ssem, rsem, device):
        return pltpu.make_async_remote_copy(
            src_ref=src, dst_ref=dst, send_sem=ssem, recv_sem=rsem,
            device_id=device, device_id_type=pl.DeviceIdType.MESH,
        )

    me = (seq, ch)
    later = ((seq + 1) % 64, ch)
    earlier = ((seq + 63) % 64, ch)
    sibling = at(y, z, 1 - k, half, x)
    pair = z + 1 - 2 * (z % 2)
    other_half = at(y, z, k, 1 - half, x)

    def along_y(d):
        return at((y + d) % NY, z, k, half, x)

    def along_z(d):
        return at(y, (z + d + NZ) % NZ, k, half, x)

    def along_x(d):
        return at(y, z, k, half, (x + d) % NX)

    def mirror(d):
        return at((y + d) % NY, z, k, 1 - half, NX - 1 - x)

    friends = [along_z(d) for d in range(1, NZ)] + [along_y(d) for d in range(1, NY)]
    friends += [along_x(d) for d in range(1, NX)] + [mirror(d) for d in range(NY)]
    friends += [later, earlier, sibling, other_half, at(y, pair, k, half, x), at(y, pair, 1 - k, half, x)]
    barrier = pltpu.get_barrier_semaphore()
    for friend in friends:
        pl.semaphore_signal(barrier, inc=1, device_id=friend, device_id_type=pl.DeviceIdType.MESH)
    pl.semaphore_wait(barrier, len(friends))

    pending = []

    def go(copy):
        copy.start()
        pending.append(copy)

    mine = (z % 2) * 2 + k
    go(send(f_ref.at[pl.ds(pl.multiple_of(mine * 64, 64), 64)], mt.at[mine], tap_ss.at[0], tap_rs.at[0], mirror(0)))
    go(send(g_ref, halo.at[0], halo_ss.at[0], halo_rs.at[0], earlier))
    go(send(g_ref, halo.at[1], halo_ss.at[1], halo_rs.at[1], later))
    for d in range(1, NY):
        go(send(p_ref, pg.at[y, z, k], py_ss.at[d - 1], py_rs.at[d - 1], along_y(d)))

    def forward(way, step, dy, src):
        sign = 1 - 2 * way
        origin = (z - sign * (step - 1) + NZ) % NZ
        slot = pg.at[(y + dy) % NY, origin, k]
        go(send(slot if src is None else src, slot, ring_ss.at[way, step - 1, dy], ring_rs.at[way, step - 1, dy], along_z(sign)))

    forward(0, 1, 0, p_ref)
    forward(1, 1, 0, p_ref)
    pg[y, z, k] = p_ref[...]

    fwd = fwd_ref[...]
    s_here[...] = dot(fwd, g_ref[...])
    s_in[...] = dot(fwd, x_ref[...])
    s_tap[...] = dot(fwd, f_ref[...])
    row = lax.broadcasted_iota(jnp.int32, (COLS, COLS), 0)
    col = lax.broadcasted_iota(jnp.int32, (COLS, COLS), 1)
    rev[...] = jnp.where(row + col == COLS - 1, 1.0, 0.0).astype(BF16)

    send(mt.at[mine], mt.at[mine], tap_ss.at[0], tap_rs.at[0], me).wait_recv()
    group = ((z, 1 - k), (pair, k), (pair, 1 - k))
    for i, (z_, k_) in enumerate(group):
        go(send(mt.at[mine], mt.at[mine], tap_ss.at[1 + i], tap_rs.at[1 + i], at(y, z_, k_, half, x)))

    for d in range(1, NY):
        slot = pg.at[(y + NY - d) % NY, z, k]
        send(slot, slot, py_ss.at[d - 1], py_rs.at[d - 1], me).wait_recv()
        forward(0, 1, NY - d, None)
        forward(1, 1, NY - d, None)

    def to_sibling(number):
        slot = pg.at[:, (z + OFFSETS[number] + NZ) % NZ, k]
        go(send(slot, slot, sib_ss.at[number], sib_rs.at[number], sibling))

    to_sibling(0)

    for i in range(2):
        send(halo.at[i], halo.at[i], halo_ss.at[i], halo_rs.at[i], me).wait_recv()
    s_next[...] = dot(fwd, halo[0])
    s_prev[...] = dot(fwd, halo[1])
    for i, (z_, k_) in enumerate(group):
        slot = mt.at[(z_ % 2) * 2 + k_]
        send(slot, slot, tap_ss.at[1 + i], tap_rs.at[1 + i], me).wait_recv()
    mirror_taps = dot(mt[...].reshape(ROWS, COLS), rev[...]).astype(BF16)
    s_mir[...] = dot(fwd, mirror_taps)

    def serve(step):
        for way in range(2):
            sign = 1 - 2 * way
            origin = (z - sign * step + NZ) % NZ
            for dy in ((0, 3, 2, 1) if step < 4 else ((0, 3) if way == 0 else (2, 1))):
                slot = pg.at[(y + dy) % NY, origin, k]
                send(slot, slot, ring_ss.at[way, step - 1, dy], ring_rs.at[way, step - 1, dy], me).wait_recv()
                if step < 3 or (step == 3 and dy in ((0, 3) if way == 0 else (2, 1))):
                    forward(way, step + 1, dy, None)
                if step == 4:
                    go(send(slot, slot, last_ss.at[dy], last_rs.at[dy], sibling))
            if step < 4:
                to_sibling(2 * step - 1 + way)

    serve(1)

    ahead = jnp.where(seq < 63, 1.0, 0.0)
    behind = jnp.where(seq > 0, 1.0, 0.0)
    even = lax.broadcasted_iota(jnp.int32, (16, COLS), 0) % 2 == 0
    up_sign = jnp.where(even, ahead, -ahead)
    dn_sign = jnp.where(even, behind, -behind)

    @pl.loop(0, ROWS // 16)
    def _(i):
        re = pl.ds(pl.multiple_of(i * 16, 16), 16)
        im = pl.ds(pl.multiple_of(ROWS + i * 16, 16), 16)
        here_r, here_i = s_here[re, :], s_here[im, :]
        up_r, up_i = here_r + up_sign * s_next[im, :], here_i - up_sign * s_next[re, :]
        dn_r, dn_i = here_r - dn_sign * s_prev[im, :], here_i + dn_sign * s_prev[re, :]
        tap_r, tap_i, mir_r, mir_i = s_tap[re, :], s_tap[im, :], s_mir[re, :], s_mir[im, :]
        in_r, in_i = s_in[re, :], s_in[im, :]
        q_conv[re, :] = (up_r * tap_r + up_i * tap_i + dn_r * mir_r - dn_i * mir_i).astype(BF16)
        q_conv[im, :] = (up_i * tap_r - up_r * tap_i + dn_r * mir_i + dn_i * mir_r).astype(BF16)
        q_pos[re, :] = (in_r * up_r + in_i * up_i).astype(BF16)
        q_pos[im, :] = (in_r * up_i - in_i * up_r).astype(BF16)
        q_neg[re, :] = (in_r * dn_r + in_i * dn_i).astype(BF16)
        q_neg[im, :] = (in_i * dn_r - in_r * dn_i).astype(BF16)

    conv = dot(inv_ref[...], q_conv[...])
    gc[...] = (conv + skip_ref[...] * g_ref[...].astype(F32)).astype(BF16)

    def x_copy(number, part):
        z_ = (z + OFFSETS[number] + NZ) % NZ
        to = 2 * part + z_ // 4
        d = (to - x + NX) % NX
        index = (d + NX - 1) % NX
        copy = send(
            sx.at[part, z_], rx.at[index, z_ % 4], xs_ss.at[number, part], xs_rs.at[index, z_ % 4], along_x(d)
        )
        return d != 0, copy

    def multiply(number):
        z_ = (z + OFFSETS[number] + NZ) % NZ
        if number < 7:
            slot = pg.at[:, z_, 1 - k]
            send(slot, slot, sib_ss.at[number], sib_rs.at[number], me).wait_recv()
        else:
            for dy in range(NY):
                slot = pg.at[(y + dy) % NY, z_, 1 - k]
                send(slot, slot, last_ss.at[dy], last_rs.at[dy], me).wait_recv()

        @pl.loop(0, NY)
        def _(y_):
            block = pg[y_, z_].reshape(128, COLS)
            part = lax.dot_general(gc[...], block, (((1,), (1,)), ((), ())), preferred_element_type=F32)
            sx[y_ % 2, z_, y_ // 2] = part.astype(BF16)

        for part in range(2):
            remote, copy = x_copy(number, part)

            @pl.when(remote)
            def _():
                copy.start()

    def chunk_sum(z_, which):
        total = sx[x // 2, z_, which].astype(F32)
        for index in range(NX - 1):
            total = total + rx[index, z_ % 4, which].astype(F32)
        return total

    def yh_copy(zq):
        return send(ysend.at[zq], yrecv.at[zq], yh_ss.at[zq], yh_rs.at[zq], other_half)

    def pass_half(number):
        z_ = (z + OFFSETS[number] + NZ) % NZ

        @pl.when(z_ // 4 == x % 2)
        def _():
            zq = z_ % 4
            for index in range(NX - 1):
                slot = rx.at[index, zq]
                send(slot, slot, xs_ss.at[0, 0], xs_rs.at[index, zq], me).wait_recv()
            ysend[zq] = chunk_sum(z_, 1 - half).astype(BF16)
            yh_copy(zq).start()

    multiply(0)

    lags[0] = dot(lag_ref[...], q_pos[...]).astype(BF16).reshape(2, NZ, 16, COLS)
    negative = dot(q_neg[...], rev[...]).astype(BF16)
    lags[1] = dot(lag_ref[...], negative).astype(BF16).reshape(2, NZ, 16, COLS)
    go(send(lags.at[:, 1 - k], kbuf, k_ss.at[0], k_rs.at[0], sibling))

    multiply(1)
    multiply(2)
    serve(2)
    send(kbuf, kbuf, k_ss.at[0], k_rs.at[0], me).wait_recv()
    for i in range(2):
        for z_ in range(NZ):
            half_sum[z_, i] = (lags[i, k, z_].astype(F32) + kbuf[i, z_].astype(F32)).astype(BF16)
    for d in range(1, NZ):
        go(send(half_sum.at[(z + d) % NZ], zbuf.at[d - 1], z_ss.at[d - 1], z_rs.at[d - 1], along_z(d)))
    pass_half(0)
    multiply(3)
    multiply(4)
    pass_half(1)
    pass_half(2)
    serve(3)
    multiply(5)
    multiply(6)
    for d in range(1, NZ):
        slot = zbuf.at[d - 1]
        send(slot, slot, z_ss.at[d - 1], z_rs.at[d - 1], me).wait_recv()
    for i in range(2):
        total = half_sum[z, i].astype(F32)
        for d in range(1, NZ):
            total = total + zbuf[d - 1, i].astype(F32)
        for y_ in range(NY):
            ysum[i, y_, 0:4] = total[4 * y_ : 4 * y_ + 4]
    for d in range(NY):
        to = (y + d) % NY
        go(send(ysum.at[1, to], yneg.at[d], y_ss.at[1, d], y_rs.at[1, d], mirror(d)))
        if d > 0:
            go(send(ysum.at[0, to], ypos.at[d - 1], y_ss.at[0, d], y_rs.at[0, d], along_y(d)))
    pass_half(3)
    pass_half(4)
    serve(4)
    multiply(7)
    pass_half(5)
    pass_half(6)

    total = ysum[0, y, 0:4]
    for d in range(NY):
        send(yneg.at[d], yneg.at[d], y_ss.at[1, d], y_rs.at[1, d], me).wait_recv()
        total = total + yneg[d, 0:4]
        if d > 0:
            send(ypos.at[d - 1], ypos.at[d - 1], y_ss.at[0, d], y_rs.at[0, d], me).wait_recv()
            total = total + ypos[d - 1, 0:4]
    fg_ref[...] = total * (1.0 / math.sqrt(16384))
    pass_half(7)

    for number in range(8):
        z_ = (z + OFFSETS[number] + NZ) % NZ

        @pl.when(z_ // 4 == x % 2)
        def _():
            zq = z_ % 4
            yh_copy(zq).wait_recv()
            value = chunk_sum(z_, half) + yrecv[zq].astype(F32)
            out_ref[:, pl.ds(pl.multiple_of(zq * 128, 128), 128)] = value.astype(BF16)

    for copy in pending:
        copy.wait_send()
    for zq in range(4):
        yh_copy(zq).wait_send()
    for number in range(8):
        for part in range(2):
            remote, copy = x_copy(number, part)

            @pl.when(remote)
            def _():
                copy.wait_send()


def body(grad_out, saved_in, filter_taps, skip_gain, projection):
    basis = half_bin_basis(ROWS)
    inverse = basis.T / ROWS

    def bf16(values):
        return jnp.asarray(values.astype(ml_dtypes.bfloat16))

    vmem, dma = pltpu.VMEM, pltpu.SemaphoreType.DMA
    square = vmem((2 * ROWS, COLS), F32)
    packed = vmem((2 * ROWS, COLS), BF16)
    scratch = [
        vmem((2, ROWS, COLS), BF16),
        vmem((4, 64, COLS), BF16),
        vmem((NY, NZ, 2, 64, COLS), BF16),
        vmem((2, NZ, 2, ROWS, 128), BF16),
        vmem((NX - 1, 4, 2, ROWS, 128), BF16),
        vmem((4, ROWS, 128), BF16),
        vmem((4, ROWS, 128), BF16),
        vmem((ROWS, COLS), BF16),
        vmem((COLS, COLS), BF16),
        square, square, square, square, square, square, packed, packed, packed,
        vmem((2, 2, NZ, 16, COLS), BF16),
        vmem((2, NZ, 16, COLS), BF16),
        vmem((NZ, 2, 16, COLS), BF16),
        vmem((NZ - 1, 2, 16, COLS), BF16),
        vmem((2, NY, 8, COLS), F32),
        vmem((NY - 1, 8, COLS), F32),
        vmem((NY, 8, COLS), F32),
        dma((4,)), dma((4,)), dma((2,)), dma((2,)), dma((3,)), dma((3,)),
        dma((2, 4, 4)), dma((2, 4, 4)), dma((7,)), dma((7,)), dma((4,)), dma((4,)),
        dma((8, 2)), dma((3, 4)), dma((4,)), dma((4,)), dma((1,)), dma((1,)),
        dma((7,)), dma((7,)), dma((2, 4)), dma((2, 4)),
    ]
    return pl.pallas_call(
        kernel,
        out_shape=(jax.ShapeDtypeStruct((ROWS, COLS), BF16), jax.ShapeDtypeStruct((4, COLS), F32)),
        in_specs=[pl.BlockSpec(memory_space=vmem)] * 8,
        out_specs=(pl.BlockSpec(memory_space=vmem), pl.BlockSpec(memory_space=vmem)),
        scratch_shapes=scratch,
        compiler_params=pltpu.CompilerParams(
            collective_id=0, has_side_effects=True, vmem_limit_bytes=48 << 20
        ),
        name="conv_backward",
    )(
        grad_out, saved_in, filter_taps, skip_gain.reshape(1, COLS), projection,
        bf16(basis), bf16(inverse), bf16(inverse[lag_order()]),
    )


def solution(mesh):
    placed = (P("seq", "ch"), P("seq", "ch"), P(None, "ch"), P("ch"), P("seq", "ch"))
    return jax.shard_map(
        body,
        mesh=mesh,
        in_specs=placed,
        out_specs=(P("seq", "ch"), P("seq", "ch")),
        check_vma=False,
    )
```

```python
import math

import jax
import jax.numpy as jnp
import ml_dtypes
import numpy as np
from jax import lax
from jax.experimental import pallas as pl
from jax.experimental.pallas import tpu as pltpu
from jax.sharding import PartitionSpec as P

NY, NZ, NX = 4, 8, 4
ROWS, COLS = 256, 512
F32, BF16 = jnp.float32, jnp.bfloat16
OFFSETS = (0, -1, 1, -2, 2, -3, 3, 4)


def half_bin_basis(rows):
    angle = np.pi * np.outer(np.arange(rows) + 0.5, np.arange(rows)) / rows
    return np.concatenate([np.cos(angle), -np.sin(angle)], axis=0)


def lag_order():
    core, y, z, r = np.meshgrid(np.arange(2), np.arange(NY), np.arange(NZ), np.arange(4), indexing="ij")
    return (((y * NZ + z) * 2 + core) * 4 + r).reshape(-1)


def dot(a, b):
    return jnp.dot(a, b, preferred_element_type=F32)


def kernel(
    g_hbm, x_hbm, f_hbm, skip_hbm, p_hbm, fwd_hbm, inv_hbm, lag_hbm,
    out_ref, fg_ref,
    g_ref, x_ref, f_ref, skip_ref, fwd_ref, inv_ref, lag_ref, in_sem,
    halo, mt, pg, sx, rx, ysend, yrecv, gc, rev,
    s_here, s_in, s_tap, s_next, s_prev, s_mir, q_conv, q_pos, q_neg,
    lags, kbuf, half_sum, ybuf, zsum, zpos, zneg,
    first_ss, tap_ss, tap_rs, halo_ss, halo_rs, py_ss, py_rs, ring_ss, ring_rs, sib_ss, sib_rs, last_ss, last_rs,
    xs_ss, xs_rs, yh_ss, yh_rs, k_ss, k_rs, y_ss, y_rs, z_ss, z_rs,
):
    seq, ch = lax.axis_index("seq"), lax.axis_index("ch")
    y, z, k = seq // 16, (seq // 2) % NZ, seq % 2
    half, x = ch // NX, ch % NX

    loads = [
        pltpu.make_async_copy(source, target, in_sem.at[i])
        for i, (source, target) in enumerate((
            (g_hbm, g_ref), (fwd_hbm, fwd_ref), (x_hbm, x_ref), (f_hbm, f_ref), (p_hbm, pg.at[y, z, k]),
            (inv_hbm, inv_ref), (lag_hbm, lag_ref), (skip_hbm, skip_ref),
        ))
    ]
    for load in loads:
        load.start()

    def at(y_, z_, k_, half_, x_):
        return ((y_ * NZ + z_) * 2 + k_, half_ * NX + x_)

    def send(src, dst, ssem, rsem, device):
        return pltpu.make_async_remote_copy(
            src_ref=src, dst_ref=dst, send_sem=ssem, recv_sem=rsem,
            device_id=device, device_id_type=pl.DeviceIdType.MESH,
        )

    me = (seq, ch)
    later = ((seq + 1) % 64, ch)
    earlier = ((seq + 63) % 64, ch)
    sibling = at(y, z, 1 - k, half, x)
    pair = z + 1 - 2 * (z % 2)
    other_half = at(y, z, k, 1 - half, x)

    def along_y(d):
        return at((y + d) % NY, z, k, half, x)

    def along_z(d):
        return at(y, (z + d + NZ) % NZ, k, half, x)

    def along_x(d):
        return at(y, z, k, half, (x + d) % NX)

    def mirror(d):
        return at(y, (z + d) % NZ, k, 1 - half, NX - 1 - x)

    friends = [along_z(d) for d in range(1, NZ)] + [along_y(d) for d in range(1, NY)]
    friends += [along_x(d) for d in range(1, NX)] + [mirror(d) for d in range(NZ)]
    friends += [later, earlier, sibling, other_half, at(y, pair, k, half, x), at(y, pair, 1 - k, half, x)]
    barrier = pltpu.get_barrier_semaphore()
    for friend in friends:
        pl.semaphore_signal(barrier, inc=1, device_id=friend, device_id_type=pl.DeviceIdType.MESH)
    source = at(3 * (1 - y // 2), z, k, 1 - half, NX - 1 - x)
    pl.semaphore_signal(barrier, inc=1, device_id=source, device_id_type=pl.DeviceIdType.MESH)
    serves = y % 3 == 0
    pl.semaphore_wait(barrier, len(friends) + jnp.where(serves, 2, 0))

    pending = []

    def go(copy):
        copy.start()
        pending.append(copy)

    mine = (z % 2) * 2 + k
    served = [
        send(
            f_hbm.at[pl.ds(pl.multiple_of(mine * 64, 64), 64)], mt.at[mine], first_ss.at[i], tap_rs.at[0],
            at(2 * (1 - y // 3) + i, z, k, 1 - half, NX - 1 - x),
        )
        for i in range(2)
    ]

    @pl.when(serves)
    def _():
        for copy in served:
            copy.start()

    go(send(g_hbm, halo.at[0], halo_ss.at[0], halo_rs.at[0], earlier))
    go(send(g_hbm, halo.at[1], halo_ss.at[1], halo_rs.at[1], later))
    def row_block(j):
        return (2 * (1 - half) + j) % NY

    def group_z(number):
        return (z + OFFSETS[number] + NZ) % NZ

    def hop(way, step, j):
        sign = 1 - 2 * way
        slot = pg.at[row_block(j), (z - sign * (step - 1) + NZ) % NZ, k]
        return send(slot, slot, ring_ss.at[way, step - 1, j], ring_rs.at[way, step - 1, j], along_z(sign))

    def arrived(way, step, j):
        slot = pg.at[row_block(j), (z - (1 - 2 * way) * step + NZ) % NZ, k]
        send(slot, slot, ring_ss.at[way, step - 1, j], ring_rs.at[way, step - 1, j], me).wait_recv()

    def to_sibling(phase, number):
        slot = pg.at[pl.ds(row_block(2 * phase), 2), group_z(number), k]
        go(send(slot, slot, sib_ss.at[phase, number], sib_rs.at[phase, number], sibling))

    def begin(phase):
        for j in (2 * phase, 2 * phase + 1):
            block = row_block(j)

            @pl.when(block != y)
            def _():
                slot = pg.at[block, z, k]
                send(slot, slot, py_ss.at[0], py_rs.at[block], me).wait_recv()
                hop(0, 1, j).start()
                hop(1, 1, j).start()

        to_sibling(phase, 0)

    own = (y + 2 + 2 * half) % NY

    def serve_own(step):
        for way in range(2):
            arrived(way, step, own)
            if step < 3:
                hop(way, step + 1, own).start()
            else:
                @pl.when(own % 2 == way)
                def _():
                    hop(way, 4, own).start()

    def serve(phase, step):
        for way in range(2):
            if step == 4:
                j = 2 * phase + way
                arrived(way, 4, j)
                slot = pg.at[row_block(j), group_z(7), k]
                go(send(slot, slot, last_ss.at[j], last_rs.at[j], sibling))
            else:
                for j in (2 * phase, 2 * phase + 1):
                    @pl.when(j != own)
                    def _():
                        arrived(way, step, j)
                        if step < 3 or j % 2 == way:
                            hop(way, step + 1, j).start()

                to_sibling(phase, 2 * step - 1 + way)

    for load in loads:
        load.wait()
    hop(0, 1, own).start()
    hop(1, 1, own).start()
    for d in range(1, NY):
        go(send(p_hbm, pg.at[y, z, k], py_ss.at[d - 1], py_rs.at[y], along_y(d)))
    fwd = fwd_ref[...]
    s_here[...] = dot(fwd, g_ref[...])
    s_in[...] = dot(fwd, x_ref[...])
    s_tap[...] = dot(fwd, f_ref[...])
    row = lax.broadcasted_iota(jnp.int32, (COLS, COLS), 0)
    col = lax.broadcasted_iota(jnp.int32, (COLS, COLS), 1)
    rev[...] = jnp.where(row + col == COLS - 1, 1.0, 0.0).astype(BF16)

    send(mt.at[mine], mt.at[mine], tap_ss.at[0], tap_rs.at[0], me).wait_recv()
    group = ((z, 1 - k), (pair, k), (pair, 1 - k))
    for i, (z_, k_) in enumerate(group):
        go(send(mt.at[mine], mt.at[mine], tap_ss.at[1 + i], tap_rs.at[1 + i], at(y, z_, k_, half, x)))

    serve_own(1)
    for i in range(2):
        send(halo.at[i], halo.at[i], halo_ss.at[i], halo_rs.at[i], me).wait_recv()
    s_next[...] = dot(fwd, halo[0])
    s_prev[...] = dot(fwd, halo[1])
    begin(0)
    begin(1)
    for i, (z_, k_) in enumerate(group):
        slot = mt.at[(z_ % 2) * 2 + k_]
        send(slot, slot, tap_ss.at[1 + i], tap_rs.at[1 + i], me).wait_recv()
    mirror_taps = dot(mt[...].reshape(ROWS, COLS), rev[...]).astype(BF16)
    s_mir[...] = dot(fwd, mirror_taps)
    serve_own(2)

    ahead = jnp.where(seq < 63, 1.0, 0.0)
    behind = jnp.where(seq > 0, 1.0, 0.0)
    even = lax.broadcasted_iota(jnp.int32, (16, COLS), 0) % 2 == 0
    up_sign = jnp.where(even, ahead, -ahead)
    dn_sign = jnp.where(even, behind, -behind)

    @pl.loop(0, ROWS // 16)
    def _(i):
        re = pl.ds(pl.multiple_of(i * 16, 16), 16)
        im = pl.ds(pl.multiple_of(ROWS + i * 16, 16), 16)
        here_r, here_i = s_here[re, :], s_here[im, :]
        up_r, up_i = here_r + up_sign * s_next[im, :], here_i - up_sign * s_next[re, :]
        dn_r, dn_i = here_r - dn_sign * s_prev[im, :], here_i + dn_sign * s_prev[re, :]
        tap_r, tap_i, mir_r, mir_i = s_tap[re, :], s_tap[im, :], s_mir[re, :], s_mir[im, :]
        in_r, in_i = s_in[re, :], s_in[im, :]
        q_conv[re, :] = (up_r * tap_r + up_i * tap_i + dn_r * mir_r - dn_i * mir_i).astype(BF16)
        q_conv[im, :] = (up_i * tap_r - up_r * tap_i + dn_r * mir_i + dn_i * mir_r).astype(BF16)
        q_pos[re, :] = (in_r * up_r + in_i * up_i).astype(BF16)
        q_pos[im, :] = (in_r * up_i - in_i * up_r).astype(BF16)
        q_neg[re, :] = (in_r * dn_r + in_i * dn_i).astype(BF16)
        q_neg[im, :] = (in_i * dn_r - in_r * dn_i).astype(BF16)

    conv = dot(inv_ref[...], q_conv[...])
    gc[...] = (conv + skip_ref[...] * g_ref[...].astype(F32)).T.astype(BF16)

    def x_copy(phase, number, part):
        z_ = group_z(number)
        d = (2 * part + z_ // 4 - x + NX) % NX
        index = (d + NX - 1) % NX
        copy = send(
            sx.at[phase, number, part], rx.at[phase, index, z_ % 4],
            xs_ss.at[phase, number, part], xs_rs.at[phase, index, z_ % 4], along_x(d),
        )
        return d != 0, copy

    def multiply(phase, number):
        z_ = group_z(number)
        if number < 7:
            slot = pg.at[pl.ds(row_block(2 * phase), 2), z_, 1 - k]
            send(slot, slot, sib_ss.at[phase, number], sib_rs.at[phase, number], me).wait_recv()
        else:
            for j in (2 * phase, 2 * phase + 1):
                slot = pg.at[row_block(j), z_, 1 - k]
                send(slot, slot, last_ss.at[j], last_rs.at[j], me).wait_recv()
        rows = pg[pl.ds(row_block(2 * phase), 2), z_].reshape(256, COLS)
        product = dot(rows, gc[...]).astype(BF16)
        for part in range(2):
            sx[phase, number, part] = product[128 * part : 128 * part + 128]
            remote, copy = x_copy(phase, number, part)

            @pl.when(remote)
            def _():
                copy.start()

    def x_sum(phase, number):
        zq = group_z(number) % 4
        total = sx[phase, number, x // 2].astype(F32)
        for index in range(NX - 1):
            slot = rx.at[phase, index, zq]
            send(slot, slot, xs_ss.at[phase, 0, 0], xs_rs.at[phase, index, zq], me).wait_recv()
            total = total + rx[phase, index, zq].astype(F32)
        return total

    def yh_copy(zq):
        return send(ysend.at[zq], yrecv.at[zq], yh_ss.at[zq], yh_rs.at[zq], other_half)

    def pass_half(number):
        @pl.when(group_z(number) // 4 == x % 2)
        def _():
            zq = group_z(number) % 4
            ysend[zq] = x_sum(0, number).astype(BF16)
            yh_copy(zq).start()

    def finish(number):
        @pl.when(group_z(number) // 4 == x % 2)
        def _():
            zq = group_z(number) % 4
            yh_copy(zq).wait_recv()
            value = x_sum(1, number) + yrecv[zq].astype(F32)
            out_ref[:, pl.ds(pl.multiple_of(zq * 128, 128), 128)] = value.T.astype(BF16)

    multiply(0, 0)

    lags[0] = dot(lag_ref[...], q_pos[...]).astype(BF16).reshape(2, NY, 32, COLS)
    negative = dot(q_neg[...], rev[...]).astype(BF16)
    lags[1] = dot(lag_ref[...], negative).astype(BF16).reshape(2, NY, 32, COLS)
    go(send(lags.at[:, 1 - k], kbuf, k_ss.at[0], k_rs.at[0], sibling))
    serve(0, 1)
    serve(1, 1)
    send(kbuf, kbuf, k_ss.at[0], k_rs.at[0], me).wait_recv()
    for i in range(2):
        for y_ in range(NY):
            half_sum[y_, i] = (lags[i, k, y_].astype(F32) + kbuf[i, y_].astype(F32)).astype(BF16)
    for d in range(1, NY):
        go(send(half_sum.at[(y + d) % NY], ybuf.at[d - 1], y_ss.at[d - 1], y_rs.at[d - 1], along_y(d)))
    serve_own(3)
    serve(0, 2)
    multiply(0, 1)
    multiply(0, 2)
    pass_half(0)
    serve(1, 2)
    serve(0, 3)
    multiply(0, 3)
    multiply(0, 4)
    pass_half(1)
    pass_half(2)
    serve(1, 3)
    multiply(1, 0)
    serve(0, 4)
    multiply(0, 5)
    multiply(0, 6)
    for d in range(1, NY):
        slot = ybuf.at[d - 1]
        send(slot, slot, y_ss.at[d - 1], y_rs.at[d - 1], me).wait_recv()
    for i in range(2):
        total = half_sum[y, i].astype(F32)
        for d in range(1, NY):
            total = total + ybuf[d - 1, i].astype(F32)
        for z_ in range(NZ):
            zsum[i, z_] = total[4 * z_ : 4 * z_ + 4]
    for d in range(NZ):
        to = (z + d) % NZ
        go(send(zsum.at[1, to], zneg.at[d], z_ss.at[1, d], z_rs.at[1, d], mirror(d)))
        if d > 0:
            go(send(zsum.at[0, to], zpos.at[d - 1], z_ss.at[0, d], z_rs.at[0, d], along_z(d)))
    multiply(1, 1)
    multiply(1, 2)
    pass_half(3)
    pass_half(4)
    serve(1, 4)
    multiply(0, 7)
    multiply(1, 3)
    multiply(1, 4)
    multiply(1, 5)
    multiply(1, 6)
    multiply(1, 7)
    pass_half(5)
    pass_half(6)
    pass_half(7)
    finish(0)
    finish(1)
    finish(2)
    finish(3)
    finish(4)
    finish(5)
    finish(6)
    total = zsum[0, z]
    for d in range(NZ):
        send(zneg.at[d], zneg.at[d], z_ss.at[1, d], z_rs.at[1, d], me).wait_recv()
        total = total + zneg[d]
        if d > 0:
            send(zpos.at[d - 1], zpos.at[d - 1], z_ss.at[0, d], z_rs.at[0, d], me).wait_recv()
            total = total + zpos[d - 1]
    fg_ref[...] = total * (1.0 / math.sqrt(16384))
    finish(7)

    @pl.when(serves)
    def _():
        for copy in served:
            copy.wait_send()

    for j in range(NY):
        for way in range(2):
            for step in (1, 2, 3, 4) if j % 2 == way else (1, 2, 3):
                hop(way, step, j).wait_send()
    for copy in pending:
        copy.wait_send()
    for zq in range(4):
        yh_copy(zq).wait_send()
    for phase in range(2):
        for number in range(8):
            for part in range(2):
                remote, copy = x_copy(phase, number, part)

                @pl.when(remote)
                def _():
                    copy.wait_send()


def body(grad_out, saved_in, filter_taps, skip_gain, projection):
    basis = half_bin_basis(ROWS)
    inverse = basis.T / ROWS

    def bf16(values):
        return jnp.asarray(values.astype(ml_dtypes.bfloat16))

    vmem, dma = pltpu.VMEM, pltpu.SemaphoreType.DMA
    square = vmem((2 * ROWS, COLS), F32)
    packed = vmem((2 * ROWS, COLS), BF16)
    block = vmem((ROWS, COLS), BF16)
    scratch = [
        block, block, block, vmem((1, COLS), F32), vmem((2 * ROWS, ROWS), BF16), block, block, dma((8,)),
        vmem((2, ROWS, COLS), BF16),
        vmem((4, 64, COLS), BF16),
        vmem((NY, NZ, 2, 64, COLS), BF16),
        vmem((2, NZ, 2, 128, ROWS), BF16),
        vmem((2, NX - 1, 4, 128, ROWS), BF16),
        vmem((4, 128, ROWS), BF16),
        vmem((4, 128, ROWS), BF16),
        vmem((COLS, ROWS), BF16),
        vmem((COLS, COLS), BF16),
        square, square, square, square, square, square, packed, packed, packed,
        vmem((2, 2, NY, 32, COLS), BF16),
        vmem((2, NY, 32, COLS), BF16),
        vmem((NY, 2, 32, COLS), BF16),
        vmem((NY - 1, 2, 32, COLS), BF16),
        vmem((2, NZ, 4, COLS), F32),
        vmem((NZ - 1, 4, COLS), F32),
        vmem((NZ, 4, COLS), F32),
        dma((2,)), dma((4,)), dma((4,)), dma((2,)), dma((2,)), dma((3,)), dma((4,)),
        dma((2, 4, 4)), dma((2, 4, 4)), dma((2, 7)), dma((2, 7)), dma((4,)), dma((4,)),
        dma((2, 8, 2)), dma((2, 3, 4)), dma((4,)), dma((4,)), dma((1,)), dma((1,)),
        dma((3,)), dma((3,)), dma((2, 8)), dma((2, 8)),
    ]
    return pl.pallas_call(
        kernel,
        out_shape=(jax.ShapeDtypeStruct((ROWS, COLS), BF16), jax.ShapeDtypeStruct((4, COLS), F32)),
        in_specs=[pl.BlockSpec(memory_space=pltpu.HBM)] * 8,
        out_specs=(pl.BlockSpec(memory_space=vmem), pl.BlockSpec(memory_space=vmem)),
        scratch_shapes=scratch,
        compiler_params=pltpu.CompilerParams(
            collective_id=0, has_side_effects=True, vmem_limit_bytes=63 << 20
        ),
        name="conv_backward",
    )(
        grad_out, saved_in, filter_taps, skip_gain.reshape(1, COLS), projection,
        bf16(basis), bf16(inverse), bf16(inverse[lag_order()]),
    )


def solution(mesh):
    placed = (P("seq", "ch"), P("seq", "ch"), P(None, "ch"), P("ch"), P("seq", "ch"))
    return jax.shard_map(
        body,
        mesh=mesh,
        in_specs=placed,
        out_specs=(P("seq", "ch"), P("seq", "ch")),
        check_vma=False,
    )
```

```python
import math

import jax
import jax.numpy as jnp
import ml_dtypes
import numpy as np
from jax import lax
from jax.experimental import pallas as pl
from jax.experimental.pallas import tpu as pltpu
from jax.sharding import PartitionSpec as P

NY, NZ, NX = 4, 8, 4
ROWS, COLS = 256, 512
F32, BF16 = jnp.float32, jnp.bfloat16
OFFSETS = (0, -1, 1, -2, 2, -3, 3, 4)


def half_bin_basis(rows):
    angle = np.pi * np.outer(np.arange(rows) + 0.5, np.arange(rows)) / rows
    return np.concatenate([np.cos(angle), -np.sin(angle)], axis=0)


def lag_order():
    core, y, z, r = np.meshgrid(np.arange(2), np.arange(NY), np.arange(NZ), np.arange(4), indexing="ij")
    return (((y * NZ + z) * 2 + core) * 4 + r).reshape(-1)


def dot(a, b):
    return jnp.dot(a, b, preferred_element_type=F32)


def kernel(
    g_hbm, x_hbm, f_hbm, skip_hbm, p_hbm, fwd_hbm, inv_hbm, lag_hbm,
    out_ref, fg_ref,
    g_ref, x_ref, f_ref, skip_ref, fwd_ref, inv_ref, lag_ref, in_sem,
    halo, mt, pg, sx, rx, ysend, yrecv, gc, rev,
    s_here, s_in, s_tap, s_next, s_prev, s_mir, q_conv, q_pos, q_neg,
    lags, kbuf, half_sum, ybuf, zsum, zpos, zneg,
    first_ss, tap_ss, tap_rs, halo_ss, halo_rs, py_ss, py_rs, ring_ss, ring_rs, sib_ss, sib_rs, last_ss, last_rs,
    xs_ss, xs_rs, yh_ss, yh_rs, k_ss, k_rs, y_ss, y_rs, z_ss, z_rs,
):
    seq, ch = lax.axis_index("seq"), lax.axis_index("ch")
    y, z, k = seq // 16, (seq // 2) % NZ, seq % 2
    half, x = ch // NX, ch % NX

    loads = [
        pltpu.make_async_copy(source, target, in_sem.at[i])
        for i, (source, target) in enumerate((
            (g_hbm, g_ref), (fwd_hbm, fwd_ref), (x_hbm, x_ref), (f_hbm, f_ref), (p_hbm, pg.at[y, z, k]),
            (inv_hbm, inv_ref), (lag_hbm, lag_ref), (skip_hbm, skip_ref),
        ))
    ]
    for load in loads:
        load.start()

    def at(y_, z_, k_, half_, x_):
        return ((y_ * NZ + z_) * 2 + k_, half_ * NX + x_)

    def send(src, dst, ssem, rsem, device):
        return pltpu.make_async_remote_copy(
            src_ref=src, dst_ref=dst, send_sem=ssem, recv_sem=rsem,
            device_id=device, device_id_type=pl.DeviceIdType.MESH,
        )

    me = (seq, ch)
    later = ((seq + 1) % 64, ch)
    earlier = ((seq + 63) % 64, ch)
    sibling = at(y, z, 1 - k, half, x)
    pair = z + 1 - 2 * (z % 2)
    other_half = at(y, z, k, 1 - half, x)

    def along_y(d):
        return at((y + d) % NY, z, k, half, x)

    def along_z(d):
        return at(y, (z + d + NZ) % NZ, k, half, x)

    def along_x(d):
        return at(y, z, k, half, (x + d) % NX)

    def mirror(d):
        return at(y, (z + d) % NZ, k, 1 - half, NX - 1 - x)

    friends = [along_z(d) for d in range(1, NZ)] + [along_y(d) for d in range(1, NY)]
    friends += [along_x(d) for d in range(1, NX)] + [mirror(d) for d in range(NZ)]
    friends += [later, earlier, sibling, other_half, at(y, pair, k, half, x), at(y, pair, 1 - k, half, x)]
    barrier = pltpu.get_barrier_semaphore()
    for friend in friends:
        pl.semaphore_signal(barrier, inc=1, device_id=friend, device_id_type=pl.DeviceIdType.MESH)
    source = at(3 * (1 - y // 2), z, k, 1 - half, NX - 1 - x)
    pl.semaphore_signal(barrier, inc=1, device_id=source, device_id_type=pl.DeviceIdType.MESH)
    serves = y % 3 == 0
    pl.semaphore_wait(barrier, len(friends) + jnp.where(serves, 2, 0))

    pending = []

    def go(copy):
        copy.start()
        pending.append(copy)

    mine = (z % 2) * 2 + k
    served = [
        send(
            f_hbm.at[pl.ds(pl.multiple_of(mine * 64, 64), 64)], mt.at[mine], first_ss.at[i], tap_rs.at[0],
            at(2 * (1 - y // 3) + i, z, k, 1 - half, NX - 1 - x),
        )
        for i in range(2)
    ]

    @pl.when(serves)
    def _():
        for copy in served:
            copy.start()

    go(send(g_hbm, halo.at[0], halo_ss.at[0], halo_rs.at[0], earlier))
    go(send(g_hbm, halo.at[1], halo_ss.at[1], halo_rs.at[1], later))
    def row_block(j):
        return (2 * (1 - half) + j) % NY

    def group_z(number):
        return (z + OFFSETS[number] + NZ) % NZ

    def hop(way, step, j):
        sign = 1 - 2 * way
        slot = pg.at[row_block(j), (z - sign * (step - 1) + NZ) % NZ, k]
        return send(slot, slot, ring_ss.at[way, step - 1, j], ring_rs.at[way, step - 1, j], along_z(sign))

    def arrived(way, step, j):
        slot = pg.at[row_block(j), (z - (1 - 2 * way) * step + NZ) % NZ, k]
        send(slot, slot, ring_ss.at[way, step - 1, j], ring_rs.at[way, step - 1, j], me).wait_recv()

    def to_sibling(phase, number):
        slot = pg.at[pl.ds(row_block(2 * phase), 2), group_z(number), k]
        go(send(slot, slot, sib_ss.at[phase, number], sib_rs.at[phase, number], sibling))

    def begin(phase):
        for j in (2 * phase, 2 * phase + 1):
            block = row_block(j)

            @pl.when(block != y)
            def _():
                slot = pg.at[block, z, k]
                send(slot, slot, py_ss.at[0], py_rs.at[block], me).wait_recv()
                hop(0, 1, j).start()
                hop(1, 1, j).start()

        to_sibling(phase, 0)

    own = (y + 2 + 2 * half) % NY

    def serve_own(step):
        for way in range(2):
            arrived(way, step, own)
            if step < 3:
                hop(way, step + 1, own).start()
            else:
                @pl.when(own % 2 == way)
                def _():
                    hop(way, 4, own).start()

    def serve(phase, step):
        for way in range(2):
            if step == 4:
                j = 2 * phase + way
                arrived(way, 4, j)
                slot = pg.at[row_block(j), group_z(7), k]
                go(send(slot, slot, last_ss.at[j], last_rs.at[j], sibling))
            else:
                for j in (2 * phase, 2 * phase + 1):
                    @pl.when(j != own)
                    def _():
                        arrived(way, step, j)
                        if step < 3 or j % 2 == way:
                            hop(way, step + 1, j).start()

                to_sibling(phase, 2 * step - 1 + way)

    for load in loads:
        load.wait()
    hop(0, 1, own).start()
    hop(1, 1, own).start()
    for d in range(1, NY):
        go(send(p_hbm, pg.at[y, z, k], py_ss.at[d - 1], py_rs.at[y], along_y(d)))
    fwd = fwd_ref[...]
    s_here[...] = dot(fwd, g_ref[...])
    s_in[...] = dot(fwd, x_ref[...])
    s_tap[...] = dot(fwd, f_ref[...])
    row = lax.broadcasted_iota(jnp.int32, (COLS, COLS), 0)
    col = lax.broadcasted_iota(jnp.int32, (COLS, COLS), 1)
    rev[...] = jnp.where(row + col == COLS - 1, 1.0, 0.0).astype(BF16)

    send(mt.at[mine], mt.at[mine], tap_ss.at[0], tap_rs.at[0], me).wait_recv()
    group = ((z, 1 - k), (pair, k), (pair, 1 - k))
    for i, (z_, k_) in enumerate(group):
        go(send(mt.at[mine], mt.at[mine], tap_ss.at[1 + i], tap_rs.at[1 + i], at(y, z_, k_, half, x)))

    serve_own(1)
    for i in range(2):
        send(halo.at[i], halo.at[i], halo_ss.at[i], halo_rs.at[i], me).wait_recv()
    s_next[...] = dot(fwd, halo[0])
    s_prev[...] = dot(fwd, halo[1])
    begin(0)
    begin(1)
    for i, (z_, k_) in enumerate(group):
        slot = mt.at[(z_ % 2) * 2 + k_]
        send(slot, slot, tap_ss.at[1 + i], tap_rs.at[1 + i], me).wait_recv()
    mirror_taps = dot(mt[...].reshape(ROWS, COLS), rev[...]).astype(BF16)
    s_mir[...] = dot(fwd, mirror_taps)
    serve_own(2)

    ahead = jnp.where(seq < 63, 1.0, 0.0)
    behind = jnp.where(seq > 0, 1.0, 0.0)
    even = lax.broadcasted_iota(jnp.int32, (16, COLS), 0) % 2 == 0
    up_sign = jnp.where(even, ahead, -ahead)
    dn_sign = jnp.where(even, behind, -behind)

    @pl.loop(0, ROWS // 16)
    def _(i):
        re = pl.ds(pl.multiple_of(i * 16, 16), 16)
        im = pl.ds(pl.multiple_of(ROWS + i * 16, 16), 16)
        here_r, here_i = s_here[re, :], s_here[im, :]
        up_r, up_i = here_r + up_sign * s_next[im, :], here_i - up_sign * s_next[re, :]
        dn_r, dn_i = here_r - dn_sign * s_prev[im, :], here_i + dn_sign * s_prev[re, :]
        tap_r, tap_i, mir_r, mir_i = s_tap[re, :], s_tap[im, :], s_mir[re, :], s_mir[im, :]
        in_r, in_i = s_in[re, :], s_in[im, :]
        q_conv[re, :] = (up_r * tap_r + up_i * tap_i + dn_r * mir_r - dn_i * mir_i).astype(BF16)
        q_conv[im, :] = (up_i * tap_r - up_r * tap_i + dn_r * mir_i + dn_i * mir_r).astype(BF16)
        q_pos[re, :] = (in_r * up_r + in_i * up_i).astype(BF16)
        q_pos[im, :] = (in_r * up_i - in_i * up_r).astype(BF16)
        q_neg[re, :] = (in_r * dn_r + in_i * dn_i).astype(BF16)
        q_neg[im, :] = (in_i * dn_r - in_r * dn_i).astype(BF16)

    conv = dot(inv_ref[...], q_conv[...])
    gc[...] = (conv + skip_ref[...] * g_ref[...].astype(F32)).T.astype(BF16)

    def x_copy(phase, number, part):
        z_ = group_z(number)
        d = (2 * part + z_ // 4 - x + NX) % NX
        index = (d + NX - 1) % NX
        copy = send(
            sx.at[phase, number, part], rx.at[phase, index, z_ % 4],
            xs_ss.at[phase, number, part], xs_rs.at[phase, index, z_ % 4], along_x(d),
        )
        return d != 0, copy

    def multiply(phase, number):
        z_ = group_z(number)
        if number < 7:
            slot = pg.at[pl.ds(row_block(2 * phase), 2), z_, 1 - k]
            send(slot, slot, sib_ss.at[phase, number], sib_rs.at[phase, number], me).wait_recv()
        else:
            for j in (2 * phase, 2 * phase + 1):
                slot = pg.at[row_block(j), z_, 1 - k]
                send(slot, slot, last_ss.at[j], last_rs.at[j], me).wait_recv()
        rows = pg[pl.ds(row_block(2 * phase), 2), z_].reshape(256, COLS)
        product = dot(rows, gc[...]).astype(BF16)
        for part in range(2):
            sx[phase, number, part] = product[128 * part : 128 * part + 128]
            remote, copy = x_copy(phase, number, part)

            @pl.when(remote)
            def _():
                copy.start()

    def x_sum(phase, number):
        zq = group_z(number) % 4
        total = sx[phase, number, x // 2].astype(F32)
        for index in range(NX - 1):
            slot = rx.at[phase, index, zq]
            send(slot, slot, xs_ss.at[phase, 0, 0], xs_rs.at[phase, index, zq], me).wait_recv()
            total = total + rx[phase, index, zq].astype(F32)
        return total

    def yh_copy(zq):
        return send(ysend.at[zq], yrecv.at[zq], yh_ss.at[zq], yh_rs.at[zq], other_half)

    def pass_half(number):
        @pl.when(group_z(number) // 4 == x % 2)
        def _():
            zq = group_z(number) % 4
            ysend[zq] = x_sum(0, number).astype(BF16)
            yh_copy(zq).start()

    def finish(number):
        @pl.when(group_z(number) // 4 == x % 2)
        def _():
            zq = group_z(number) % 4
            yh_copy(zq).wait_recv()
            value = x_sum(1, number) + yrecv[zq].astype(F32)
            out_ref[:, pl.ds(pl.multiple_of(zq * 128, 128), 128)] = value.T.astype(BF16)

    multiply(0, 0)
    multiply(1, 0)
    serve(0, 1)
    serve(1, 1)

    lags[0] = dot(lag_ref[...], q_pos[...]).astype(BF16).reshape(2, NY, 32, COLS)
    negative = dot(q_neg[...], rev[...]).astype(BF16)
    lags[1] = dot(lag_ref[...], negative).astype(BF16).reshape(2, NY, 32, COLS)
    go(send(lags.at[:, 1 - k], kbuf, k_ss.at[0], k_rs.at[0], sibling))
    serve_own(3)
    multiply(0, 1)
    multiply(0, 2)
    serve(0, 2)
    send(kbuf, kbuf, k_ss.at[0], k_rs.at[0], me).wait_recv()
    for i in range(2):
        for y_ in range(NY):
            half_sum[y_, i] = (lags[i, k, y_].astype(F32) + kbuf[i, y_].astype(F32)).astype(BF16)
    for d in range(1, NY):
        go(send(half_sum.at[(y + d) % NY], ybuf.at[d - 1], y_ss.at[d - 1], y_rs.at[d - 1], along_y(d)))
    serve(1, 2)
    multiply(0, 3)
    multiply(0, 4)
    pass_half(0)
    serve(0, 3)
    serve(1, 3)
    pass_half(1)
    pass_half(2)
    multiply(0, 5)
    multiply(0, 6)
    serve(0, 4)
    serve(1, 4)
    multiply(0, 7)
    multiply(1, 1)
    multiply(1, 2)
    multiply(1, 3)
    multiply(1, 4)
    multiply(1, 5)
    multiply(1, 6)
    multiply(1, 7)
    pass_half(3)
    pass_half(4)
    for d in range(1, NY):
        slot = ybuf.at[d - 1]
        send(slot, slot, y_ss.at[d - 1], y_rs.at[d - 1], me).wait_recv()
    for i in range(2):
        total = half_sum[y, i].astype(F32)
        for d in range(1, NY):
            total = total + ybuf[d - 1, i].astype(F32)
        for z_ in range(NZ):
            zsum[i, z_] = total[4 * z_ : 4 * z_ + 4]
    for d in range(NZ):
        to = (z + d) % NZ
        go(send(zsum.at[1, to], zneg.at[d], z_ss.at[1, d], z_rs.at[1, d], mirror(d)))
        if d > 0:
            go(send(zsum.at[0, to], zpos.at[d - 1], z_ss.at[0, d], z_rs.at[0, d], along_z(d)))
    pass_half(5)
    pass_half(6)
    pass_half(7)
    finish(0)
    finish(1)
    finish(2)
    finish(3)
    finish(4)
    finish(5)
    finish(6)
    total = zsum[0, z]
    for d in range(NZ):
        send(zneg.at[d], zneg.at[d], z_ss.at[1, d], z_rs.at[1, d], me).wait_recv()
        total = total + zneg[d]
        if d > 0:
            send(zpos.at[d - 1], zpos.at[d - 1], z_ss.at[0, d], z_rs.at[0, d], me).wait_recv()
            total = total + zpos[d - 1]
    fg_ref[...] = total * (1.0 / math.sqrt(16384))
    finish(7)

    @pl.when(serves)
    def _():
        for copy in served:
            copy.wait_send()

    for j in range(NY):
        for way in range(2):
            for step in (1, 2, 3, 4) if j % 2 == way else (1, 2, 3):
                hop(way, step, j).wait_send()
    for copy in pending:
        copy.wait_send()
    for zq in range(4):
        yh_copy(zq).wait_send()
    for phase in range(2):
        for number in range(8):
            for part in range(2):
                remote, copy = x_copy(phase, number, part)

                @pl.when(remote)
                def _():
                    copy.wait_send()


def body(grad_out, saved_in, filter_taps, skip_gain, projection):
    basis = half_bin_basis(ROWS)
    inverse = basis.T / ROWS

    def bf16(values):
        return jnp.asarray(values.astype(ml_dtypes.bfloat16))

    vmem, dma = pltpu.VMEM, pltpu.SemaphoreType.DMA
    square = vmem((2 * ROWS, COLS), F32)
    packed = vmem((2 * ROWS, COLS), BF16)
    block = vmem((ROWS, COLS), BF16)
    scratch = [
        block, block, block, vmem((1, COLS), F32), vmem((2 * ROWS, ROWS), BF16), block, block, dma((8,)),
        vmem((2, ROWS, COLS), BF16),
        vmem((4, 64, COLS), BF16),
        vmem((NY, NZ, 2, 64, COLS), BF16),
        vmem((2, NZ, 2, 128, ROWS), BF16),
        vmem((2, NX - 1, 4, 128, ROWS), BF16),
        vmem((4, 128, ROWS), BF16),
        vmem((4, 128, ROWS), BF16),
        vmem((COLS, ROWS), BF16),
        vmem((COLS, COLS), BF16),
        square, square, square, square, square, square, packed, packed, packed,
        vmem((2, 2, NY, 32, COLS), BF16),
        vmem((2, NY, 32, COLS), BF16),
        vmem((NY, 2, 32, COLS), BF16),
        vmem((NY - 1, 2, 32, COLS), BF16),
        vmem((2, NZ, 4, COLS), F32),
        vmem((NZ - 1, 4, COLS), F32),
        vmem((NZ, 4, COLS), F32),
        dma((2,)), dma((4,)), dma((4,)), dma((2,)), dma((2,)), dma((3,)), dma((4,)),
        dma((2, 4, 4)), dma((2, 4, 4)), dma((2, 7)), dma((2, 7)), dma((4,)), dma((4,)),
        dma((2, 8, 2)), dma((2, 3, 4)), dma((4,)), dma((4,)), dma((1,)), dma((1,)),
        dma((3,)), dma((3,)), dma((2, 8)), dma((2, 8)),
    ]
    return pl.pallas_call(
        kernel,
        out_shape=(jax.ShapeDtypeStruct((ROWS, COLS), BF16), jax.ShapeDtypeStruct((4, COLS), F32)),
        in_specs=[pl.BlockSpec(memory_space=pltpu.HBM)] * 8,
        out_specs=(pl.BlockSpec(memory_space=vmem), pl.BlockSpec(memory_space=vmem)),
        scratch_shapes=scratch,
        compiler_params=pltpu.CompilerParams(
            collective_id=0, has_side_effects=True, vmem_limit_bytes=63 << 20
        ),
        name="conv_backward",
    )(
        grad_out, saved_in, filter_taps, skip_gain.reshape(1, COLS), projection,
        bf16(basis), bf16(inverse), bf16(inverse[lag_order()]),
    )


def solution(mesh):
    placed = (P("seq", "ch"), P("seq", "ch"), P(None, "ch"), P("ch"), P("seq", "ch"))
    return jax.shard_map(
        body,
        mesh=mesh,
        in_specs=placed,
        out_specs=(P("seq", "ch"), P("seq", "ch")),
        check_vma=False,
    )
```

```python
import math

import jax
import jax.numpy as jnp
import ml_dtypes
import numpy as np
from jax import lax
from jax.experimental import pallas as pl
from jax.experimental.pallas import tpu as pltpu
from jax.sharding import PartitionSpec as P

NY, NZ, NX = 4, 8, 4
ROWS, COLS = 256, 512
F32, BF16 = jnp.float32, jnp.bfloat16
OFFSETS = (0, -1, 1, -2, 2, -3, 3, 4)


def half_bin_basis(rows):
    angle = np.pi * np.outer(np.arange(rows) + 0.5, np.arange(rows)) / rows
    return np.concatenate([np.cos(angle), -np.sin(angle)], axis=0)


def lag_order():
    core, y, z, r = np.meshgrid(np.arange(2), np.arange(NY), np.arange(NZ), np.arange(4), indexing="ij")
    return (((y * NZ + z) * 2 + core) * 4 + r).reshape(-1)


def dot(a, b):
    return jnp.dot(a, b, preferred_element_type=F32)


def kernel(
    g_hbm, x_hbm, f_hbm, skip_hbm, p_hbm, fwd_hbm, inv_hbm, lag_hbm,
    out_ref, fg_ref,
    g_ref, x_ref, f_ref, skip_ref, fwd_ref, inv_ref, lag_ref, in_sem,
    halo, mt, pg, sx, rx, ysend, yrecv, gc, rev,
    s_here, s_in, s_tap, s_next, s_prev, s_mir, q_conv, q_pos, q_neg,
    lags, kbuf, half_sum, ybuf, zsum, zpos, zneg,
    first_ss, tap_ss, tap_rs, halo_ss, halo_rs, py_ss, py_rs, ring_ss, ring_rs, sib_ss, sib_rs, last_ss, last_rs,
    xs_ss, xs_rs, yh_ss, yh_rs, k_ss, k_rs, y_ss, y_rs, z_ss, z_rs,
):
    seq, ch = lax.axis_index("seq"), lax.axis_index("ch")
    y, z, k = seq // 16, (seq // 2) % NZ, seq % 2
    half, x = ch // NX, ch % NX

    loads = [
        pltpu.make_async_copy(source, target, in_sem.at[i])
        for i, (source, target) in enumerate((
            (g_hbm, g_ref), (fwd_hbm, fwd_ref), (x_hbm, x_ref), (f_hbm, f_ref), (p_hbm, pg.at[y, z, k]),
            (inv_hbm, inv_ref), (lag_hbm, lag_ref), (skip_hbm, skip_ref),
        ))
    ]
    for load in loads:
        load.start()

    def at(y_, z_, k_, half_, x_):
        return ((y_ * NZ + z_) * 2 + k_, half_ * NX + x_)

    def send(src, dst, ssem, rsem, device):
        return pltpu.make_async_remote_copy(
            src_ref=src, dst_ref=dst, send_sem=ssem, recv_sem=rsem,
            device_id=device, device_id_type=pl.DeviceIdType.MESH,
        )

    me = (seq, ch)
    later = ((seq + 1) % 64, ch)
    earlier = ((seq + 63) % 64, ch)
    sibling = at(y, z, 1 - k, half, x)
    pair = z + 1 - 2 * (z % 2)
    other_half = at(y, z, k, 1 - half, x)

    def along_y(d):
        return at((y + d) % NY, z, k, half, x)

    def along_z(d):
        return at(y, (z + d + NZ) % NZ, k, half, x)

    def along_x(d):
        return at(y, z, k, half, (x + d) % NX)

    def mirror(d):
        return at(y, (z + d) % NZ, k, 1 - half, NX - 1 - x)

    friends = [along_z(d) for d in range(1, NZ)] + [along_y(d) for d in range(1, NY)]
    friends += [along_x(d) for d in range(1, NX)] + [mirror(d) for d in range(NZ)]
    friends += [later, earlier, sibling, other_half, at(y, pair, k, half, x), at(y, pair, 1 - k, half, x)]
    barrier = pltpu.get_barrier_semaphore()
    for friend in friends:
        pl.semaphore_signal(barrier, inc=1, device_id=friend, device_id_type=pl.DeviceIdType.MESH)
    source = at(3 * (1 - y // 2), z, k, 1 - half, NX - 1 - x)
    pl.semaphore_signal(barrier, inc=1, device_id=source, device_id_type=pl.DeviceIdType.MESH)
    serves = y % 3 == 0
    pl.semaphore_wait(barrier, len(friends) + jnp.where(serves, 2, 0))

    pending = []

    def go(copy):
        copy.start()
        pending.append(copy)

    mine = (z % 2) * 2 + k
    served = [
        send(
            f_hbm.at[pl.ds(pl.multiple_of(mine * 64, 64), 64)], mt.at[mine], first_ss.at[i], tap_rs.at[0],
            at(2 * (1 - y // 3) + i, z, k, 1 - half, NX - 1 - x),
        )
        for i in range(2)
    ]

    @pl.when(serves)
    def _():
        for copy in served:
            copy.start()

    go(send(g_hbm, halo.at[0], halo_ss.at[0], halo_rs.at[0], earlier))
    go(send(g_hbm, halo.at[1], halo_ss.at[1], halo_rs.at[1], later))
    def row_block(j):
        return (2 * (1 - half) + j) % NY

    def group_z(number):
        return (z + OFFSETS[number] + NZ) % NZ

    def hop(way, step, j):
        sign = 1 - 2 * way
        slot = pg.at[row_block(j), (z - sign * (step - 1) + NZ) % NZ, k]
        return send(slot, slot, ring_ss.at[way, step - 1, j], ring_rs.at[way, step - 1, j], along_z(sign))

    def arrived(way, step, j):
        slot = pg.at[row_block(j), (z - (1 - 2 * way) * step + NZ) % NZ, k]
        send(slot, slot, ring_ss.at[way, step - 1, j], ring_rs.at[way, step - 1, j], me).wait_recv()

    def to_sibling(phase, number):
        slot = pg.at[pl.ds(row_block(2 * phase), 2), group_z(number), k]
        go(send(slot, slot, sib_ss.at[phase, number], sib_rs.at[phase, number], sibling))

    def begin(phase):
        for j in (2 * phase, 2 * phase + 1):
            block = row_block(j)

            @pl.when(block != y)
            def _():
                slot = pg.at[block, z, k]
                send(slot, slot, py_ss.at[0], py_rs.at[block], me).wait_recv()
                hop(0, 1, j).start()
                hop(1, 1, j).start()

        to_sibling(phase, 0)

    own = (y + 2 + 2 * half) % NY

    def serve_own(step):
        for way in range(2):
            arrived(way, step, own)
            if step < 3:
                hop(way, step + 1, own).start()
            else:
                @pl.when(own % 2 == way)
                def _():
                    hop(way, 4, own).start()

    def serve(phase, step):
        for way in range(2):
            if step == 4:
                j = 2 * phase + way
                arrived(way, 4, j)
                slot = pg.at[row_block(j), group_z(7), k]
                go(send(slot, slot, last_ss.at[j], last_rs.at[j], sibling))
            else:
                for j in (2 * phase, 2 * phase + 1):
                    @pl.when(j != own)
                    def _():
                        arrived(way, step, j)
                        if step < 3 or j % 2 == way:
                            hop(way, step + 1, j).start()

                to_sibling(phase, 2 * step - 1 + way)

    for load in loads:
        load.wait()
    hop(0, 1, own).start()
    hop(1, 1, own).start()
    for d in range(1, NY):
        go(send(p_hbm, pg.at[y, z, k], py_ss.at[d - 1], py_rs.at[y], along_y(d)))
    fwd = fwd_ref[...]
    s_here[...] = dot(fwd, g_ref[...])
    s_in[...] = dot(fwd, x_ref[...])
    s_tap[...] = dot(fwd, f_ref[...])
    row = lax.broadcasted_iota(jnp.int32, (COLS, COLS), 0)
    col = lax.broadcasted_iota(jnp.int32, (COLS, COLS), 1)
    rev[...] = jnp.where(row + col == COLS - 1, 1.0, 0.0).astype(BF16)

    send(mt.at[mine], mt.at[mine], tap_ss.at[0], tap_rs.at[0], me).wait_recv()
    group = ((z, 1 - k), (pair, k), (pair, 1 - k))
    for i, (z_, k_) in enumerate(group):
        go(send(mt.at[mine], mt.at[mine], tap_ss.at[1 + i], tap_rs.at[1 + i], at(y, z_, k_, half, x)))

    serve_own(1)
    for i in range(2):
        send(halo.at[i], halo.at[i], halo_ss.at[i], halo_rs.at[i], me).wait_recv()
    s_next[...] = dot(fwd, halo[0])
    s_prev[...] = dot(fwd, halo[1])
    begin(0)
    begin(1)
    for i, (z_, k_) in enumerate(group):
        slot = mt.at[(z_ % 2) * 2 + k_]
        send(slot, slot, tap_ss.at[1 + i], tap_rs.at[1 + i], me).wait_recv()
    mirror_taps = dot(mt[...].reshape(ROWS, COLS), rev[...]).astype(BF16)
    s_mir[...] = dot(fwd, mirror_taps)
    serve_own(2)

    ahead = jnp.where(seq < 63, 1.0, 0.0)
    behind = jnp.where(seq > 0, 1.0, 0.0)
    even = lax.broadcasted_iota(jnp.int32, (16, COLS), 0) % 2 == 0
    up_sign = jnp.where(even, ahead, -ahead)
    dn_sign = jnp.where(even, behind, -behind)

    @pl.loop(0, ROWS // 16)
    def _(i):
        re = pl.ds(pl.multiple_of(i * 16, 16), 16)
        im = pl.ds(pl.multiple_of(ROWS + i * 16, 16), 16)
        here_r, here_i = s_here[re, :], s_here[im, :]
        up_r, up_i = here_r + up_sign * s_next[im, :], here_i - up_sign * s_next[re, :]
        dn_r, dn_i = here_r - dn_sign * s_prev[im, :], here_i + dn_sign * s_prev[re, :]
        tap_r, tap_i, mir_r, mir_i = s_tap[re, :], s_tap[im, :], s_mir[re, :], s_mir[im, :]
        in_r, in_i = s_in[re, :], s_in[im, :]
        q_conv[re, :] = (up_r * tap_r + up_i * tap_i + dn_r * mir_r - dn_i * mir_i).astype(BF16)
        q_conv[im, :] = (up_i * tap_r - up_r * tap_i + dn_r * mir_i + dn_i * mir_r).astype(BF16)
        q_pos[re, :] = (in_r * up_r + in_i * up_i).astype(BF16)
        q_pos[im, :] = (in_r * up_i - in_i * up_r).astype(BF16)
        q_neg[re, :] = (in_r * dn_r + in_i * dn_i).astype(BF16)
        q_neg[im, :] = (in_i * dn_r - in_r * dn_i).astype(BF16)

    conv = dot(inv_ref[...], q_conv[...])
    gc[...] = (conv + skip_ref[...] * g_ref[...].astype(F32)).T.astype(BF16)

    def x_copy(phase, number, part):
        z_ = group_z(number)
        d = (2 * part + z_ // 4 - x + NX) % NX
        index = (d + NX - 1) % NX
        copy = send(
            sx.at[phase, number, part], rx.at[phase, index, z_ % 4],
            xs_ss.at[phase, number, part], xs_rs.at[phase, index, z_ % 4], along_x(d),
        )
        return d != 0, copy

    def multiply(phase, number):
        z_ = group_z(number)
        if number < 7:
            slot = pg.at[pl.ds(row_block(2 * phase), 2), z_, 1 - k]
            send(slot, slot, sib_ss.at[phase, number], sib_rs.at[phase, number], me).wait_recv()
        else:
            for j in (2 * phase, 2 * phase + 1):
                slot = pg.at[row_block(j), z_, 1 - k]
                send(slot, slot, last_ss.at[j], last_rs.at[j], me).wait_recv()
        rows = pg[pl.ds(row_block(2 * phase), 2), z_].reshape(256, COLS)
        product = dot(rows, gc[...]).astype(BF16)
        for part in range(2):
            sx[phase, number, part] = product[128 * part : 128 * part + 128]
            remote, copy = x_copy(phase, number, part)

            @pl.when(remote)
            def _():
                copy.start()

    def x_sum(phase, number):
        zq = group_z(number) % 4
        total = sx[phase, number, x // 2].astype(F32)
        for index in range(NX - 1):
            slot = rx.at[phase, index, zq]
            send(slot, slot, xs_ss.at[phase, 0, 0], xs_rs.at[phase, index, zq], me).wait_recv()
            total = total + rx[phase, index, zq].astype(F32)
        return total

    def yh_copy(zq):
        return send(ysend.at[zq], yrecv.at[zq], yh_ss.at[zq], yh_rs.at[zq], other_half)

    def pass_half(number):
        @pl.when(group_z(number) // 4 == x % 2)
        def _():
            zq = group_z(number) % 4
            ysend[zq] = x_sum(0, number).astype(BF16)
            yh_copy(zq).start()

    def finish(number):
        @pl.when(group_z(number) // 4 == x % 2)
        def _():
            zq = group_z(number) % 4
            yh_copy(zq).wait_recv()
            value = x_sum(1, number) + yrecv[zq].astype(F32)
            out_ref[:, pl.ds(pl.multiple_of(zq * 128, 128), 128)] = value.T.astype(BF16)

    multiply(0, 0)
    multiply(1, 0)
    serve(0, 1)
    serve(1, 1)

    lags[0] = dot(lag_ref[...], q_pos[...]).astype(BF16).reshape(2, NY, 32, COLS)
    negative = dot(q_neg[...], rev[...]).astype(BF16)
    lags[1] = dot(lag_ref[...], negative).astype(BF16).reshape(2, NY, 32, COLS)
    go(send(lags.at[:, 1 - k], kbuf, k_ss.at[0], k_rs.at[0], sibling))
    serve_own(3)
    multiply(0, 1)
    multiply(0, 2)
    serve(0, 2)
    send(kbuf, kbuf, k_ss.at[0], k_rs.at[0], me).wait_recv()
    for i in range(2):
        for y_ in range(NY):
            half_sum[y_, i] = (lags[i, k, y_].astype(F32) + kbuf[i, y_].astype(F32)).astype(BF16)
    for d in range(1, NY):
        go(send(half_sum.at[(y + d) % NY], ybuf.at[d - 1], y_ss.at[d - 1], y_rs.at[d - 1], along_y(d)))
    serve(1, 2)
    multiply(0, 3)
    multiply(0, 4)
    pass_half(0)
    serve(0, 3)
    serve(1, 3)
    pass_half(1)
    pass_half(2)
    multiply(0, 5)
    multiply(0, 6)
    serve(0, 4)
    serve(1, 4)
    multiply(0, 7)
    multiply(1, 1)
    multiply(1, 2)
    multiply(1, 3)
    multiply(1, 4)
    multiply(1, 5)
    multiply(1, 6)
    multiply(1, 7)
    for d in range(1, NY):
        slot = ybuf.at[d - 1]
        send(slot, slot, y_ss.at[d - 1], y_rs.at[d - 1], me).wait_recv()
    for i in range(2):
        total = half_sum[y, i].astype(F32)
        for d in range(1, NY):
            total = total + ybuf[d - 1, i].astype(F32)
        for z_ in range(NZ):
            zsum[i, z_] = total[4 * z_ : 4 * z_ + 4]
    for d in range(NZ):
        to = (z + d) % NZ
        go(send(zsum.at[1, to], zneg.at[d], z_ss.at[1, d], z_rs.at[1, d], mirror(d)))
        if d > 0:
            go(send(zsum.at[0, to], zpos.at[d - 1], z_ss.at[0, d], z_rs.at[0, d], along_z(d)))
    pass_half(3)
    pass_half(4)
    pass_half(5)
    pass_half(6)
    pass_half(7)
    finish(0)
    finish(1)
    finish(2)
    finish(3)
    finish(4)
    finish(5)
    finish(6)
    total = zsum[0, z]
    for d in range(NZ):
        send(zneg.at[d], zneg.at[d], z_ss.at[1, d], z_rs.at[1, d], me).wait_recv()
        total = total + zneg[d]
        if d > 0:
            send(zpos.at[d - 1], zpos.at[d - 1], z_ss.at[0, d], z_rs.at[0, d], me).wait_recv()
            total = total + zpos[d - 1]
    fg_ref[...] = total * (1.0 / math.sqrt(16384))
    finish(7)

    @pl.when(serves)
    def _():
        for copy in served:
            copy.wait_send()

    for j in range(NY):
        for way in range(2):
            for step in (1, 2, 3, 4) if j % 2 == way else (1, 2, 3):
                hop(way, step, j).wait_send()
    for copy in pending:
        copy.wait_send()
    for zq in range(4):
        yh_copy(zq).wait_send()
    for phase in range(2):
        for number in range(8):
            for part in range(2):
                remote, copy = x_copy(phase, number, part)

                @pl.when(remote)
                def _():
                    copy.wait_send()


def body(grad_out, saved_in, filter_taps, skip_gain, projection):
    basis = half_bin_basis(ROWS)
    inverse = basis.T / ROWS

    def bf16(values):
        return jnp.asarray(values.astype(ml_dtypes.bfloat16))

    vmem, dma = pltpu.VMEM, pltpu.SemaphoreType.DMA
    square = vmem((2 * ROWS, COLS), F32)
    packed = vmem((2 * ROWS, COLS), BF16)
    block = vmem((ROWS, COLS), BF16)
    scratch = [
        block, block, block, vmem((1, COLS), F32), vmem((2 * ROWS, ROWS), BF16), block, block, dma((8,)),
        vmem((2, ROWS, COLS), BF16),
        vmem((4, 64, COLS), BF16),
        vmem((NY, NZ, 2, 64, COLS), BF16),
        vmem((2, NZ, 2, 128, ROWS), BF16),
        vmem((2, NX - 1, 4, 128, ROWS), BF16),
        vmem((4, 128, ROWS), BF16),
        vmem((4, 128, ROWS), BF16),
        vmem((COLS, ROWS), BF16),
        vmem((COLS, COLS), BF16),
        square, square, square, square, square, square, packed, packed, packed,
        vmem((2, 2, NY, 32, COLS), BF16),
        vmem((2, NY, 32, COLS), BF16),
        vmem((NY, 2, 32, COLS), BF16),
        vmem((NY - 1, 2, 32, COLS), BF16),
        vmem((2, NZ, 4, COLS), F32),
        vmem((NZ - 1, 4, COLS), F32),
        vmem((NZ, 4, COLS), F32),
        dma((2,)), dma((4,)), dma((4,)), dma((2,)), dma((2,)), dma((3,)), dma((4,)),
        dma((2, 4, 4)), dma((2, 4, 4)), dma((2, 7)), dma((2, 7)), dma((4,)), dma((4,)),
        dma((2, 8, 2)), dma((2, 3, 4)), dma((4,)), dma((4,)), dma((1,)), dma((1,)),
        dma((3,)), dma((3,)), dma((2, 8)), dma((2, 8)),
    ]
    return pl.pallas_call(
        kernel,
        out_shape=(jax.ShapeDtypeStruct((ROWS, COLS), BF16), jax.ShapeDtypeStruct((4, COLS), F32)),
        in_specs=[pl.BlockSpec(memory_space=pltpu.HBM)] * 8,
        out_specs=(pl.BlockSpec(memory_space=vmem), pl.BlockSpec(memory_space=vmem)),
        scratch_shapes=scratch,
        compiler_params=pltpu.CompilerParams(
            collective_id=0, has_side_effects=True, vmem_limit_bytes=63 << 20
        ),
        name="conv_backward",
    )(
        grad_out, saved_in, filter_taps, skip_gain.reshape(1, COLS), projection,
        bf16(basis), bf16(inverse), bf16(inverse[lag_order()]),
    )


def solution(mesh):
    placed = (P("seq", "ch"), P("seq", "ch"), P(None, "ch"), P("ch"), P("seq", "ch"))
    return jax.shard_map(
        body,
        mesh=mesh,
        in_specs=placed,
        out_specs=(P("seq", "ch"), P("seq", "ch")),
        check_vma=False,
    )
```
